32 devices in a mesh: clip: 4 (over y, core), seq: 8 (over z, x).
Axes of the slice: x: 2, y: 2, z: 4, core: 2. Of those that a mesh axis runs over, the one named last changes fastest.
Arguments:
- temporal_queries: bfloat16 [32, 128, 1152], P(('clip', 'seq')), parts along dimension 0, may hold values from -6 to 6
- temporal_keys: bfloat16 [32, 128, 1152], P(('clip', 'seq')), parts along dimension 0, may hold values from -6 to 6
- temporal_values: bfloat16 [32, 128, 1152], P(('clip', 'seq')), parts along dimension 0, may hold values from -6 to 6
- temporal_cotangent: bfloat16 [32, 128, 1152], P(('clip', 'seq')), parts along dimension 0, may hold values from -6 to 6
- cross_queries: bfloat16 [32, 128, 1152], P(('clip', 'seq')), parts along dimension 0, may hold values from -6 to 6
- cross_cotangent: bfloat16 [32, 128, 1152], P(('clip', 'seq')), parts along dimension 0, may hold values from -6 to 6
- text_keys: bfloat16 [640, 1152], P('clip'), parts along dimension 0, may hold values from -6 to 6
- text_values: bfloat16 [640, 1152], P('clip'), parts along dimension 0, may hold values from -6 to 6
- text_length: int32 [4], P('clip'), parts along dimension 0, may hold values from 80 to 160
Outputs:
- temporal_queries_grad: bfloat16 [32, 128, 1152], P(('clip', 'seq')), parts along dimension 0
- temporal_keys_grad: bfloat16 [32, 128, 1152], P(('clip', 'seq')), parts along dimension 0
- temporal_values_grad: bfloat16 [32, 128, 1152], P(('clip', 'seq')), parts along dimension 0
- cross_queries_grad: bfloat16 [32, 128, 1152], P(('clip', 'seq')), parts along dimension 0
- text_kv_grad: float32 [640, 2304], P('clip', 'seq'), parts along dimension 0
The draws below stay inside these ranges and needn't reach their ends.
There are 4 independent parts, one for each index of `clip`. The reference program is written for one: setup_inputs(seed, part) draws one part's arguments, and reference() takes and returns one part's arrays. A program takes and returns all parts, laid end to end along the dimension named above; each array names one. Nothing has to cross between parts.
All inputs are finite; a program needn't handle non-finite values.
Results may differ from the reference program's by a relative error of at most 0.012.
The reference program's roundings to bfloat16 on the way count: a program that leaves them out, or rounds other values in their place, can miss the bound.
Values may be sent and summed in bfloat16 or wider, within the bound.
No kernel may reach another device: no remote copies, remote signals or barrier semaphores. Data moves between devices by JAX's collectives and lax.ppermute only.
A program may use at most 64 MiB of HBM per device.

```python
import math
import jax
import jax.numpy as jnp
from jax import lax

D = 1152
HEADS = 16
TEXT = 160
HEAD_DIM = 72
POS = 128
FRAMES = 8


def base_field(key, extent):
    return jnp.clip(jax.random.normal(key, extent, jnp.float32), -6.0, 6.0)


def temporal_pair(key):
    key_query, key_target = jax.random.split(jax.random.fold_in(key, 101), 2)
    queries = base_field(key_query, (FRAMES, POS, D))
    targets = base_field(key_target, (FRAMES, POS, D))
    return (queries, targets)


def cross_pair(key):
    key_query, key_target = jax.random.split(jax.random.fold_in(key, 202), 2)
    queries = base_field(key_query, (FRAMES, POS, D))
    targets = base_field(key_target, (TEXT, D))
    return (queries, targets)


def draw_temporal_queries(key, part):
    return temporal_pair(key)[0].astype(jnp.bfloat16)


def draw_temporal_keys(key, part):
    return temporal_pair(key)[1].astype(jnp.bfloat16)


def draw_cross_queries(key, part):
    return cross_pair(key)[0].astype(jnp.bfloat16)


def draw_text_keys(key, part):
    return cross_pair(key)[1].astype(jnp.bfloat16)


def raised(values, rng, source, target, shards_of, factor):
    owner, partner = [(jnp.arange(values.shape[axis_at]) // (values.shape[axis_at] // shards_of)).reshape([-1 if axis == axis_at else 1 for axis in range(values.ndim)]) for axis_at in (source, target)]
    chosen = jax.random.permutation(rng, shards_of)[partner]
    strong = (owner == chosen) | (owner == (partner + shards_of // 2) % shards_of)
    return jnp.where(strong, factor * values, values)


def steps_of(own_key, dims, cuts, least, top_value):
    def one(dim, blocks):
        steps = jax.random.uniform(jax.random.fold_in(jax.random.fold_in(own_key, 6), dim), (blocks,), jnp.float32, least / len(cuts), top_value / len(cuts))
        return jnp.repeat(jnp.exp(steps), dims[dim] // blocks).reshape((-1,) + (1,) * (len(dims) - dim - 1))

    loudness = one(*cuts[0])
    for cut in cuts[1:]:
        loudness = loudness * one(*cut)
    return loudness


def scatter_about(rng, shape, deviation, bound, shards=(), kind=jnp.bfloat16):
    entries = jax.random.normal(rng, shape, jnp.float32) * deviation
    if len(shards) > 0:
        entries = steps_of(rng, shape, shards, -0.22, 0.18) * entries
    return jnp.clip(entries, min=-bound, max=bound).astype(kind)


def gaussian_with(key, shape, scale, reach, cuts, heavy, kind=jnp.bfloat16):
    values = scale * jax.random.normal(key, shape, jnp.float32)
    if cuts:
        values = values * steps_of(key, shape, cuts, -0.22, 0.18)
    return jnp.clip(raised(values, jax.random.fold_in(key, 3), *heavy), -reach, reach).astype(kind)


def setup_inputs(seed: int = 0, part: int = 0) -> dict:
    splits = jax.random.split(jax.random.key(seed), 10)
    part_keys = jax.random.split(jax.random.fold_in(splits[9], part), 10)
    temporal_queries = draw_temporal_queries(jax.random.fold_in(jax.random.fold_in(splits[9], part), 71), part)
    temporal_keys = draw_temporal_keys(jax.random.fold_in(jax.random.fold_in(splits[9], part), 71), part)
    temporal_values = scatter_about(part_keys[2], (FRAMES, POS, D), 1.0, 6.0, ((0, 8),))
    temporal_cotangent = scatter_about(part_keys[3], (FRAMES, POS, D), 1.0, 6.0, ((0, 8),))
    cross_queries = draw_cross_queries(jax.random.fold_in(jax.random.fold_in(splits[9], part), 71), part)
    cross_cotangent = gaussian_with(part_keys[5], (FRAMES, POS, D), 1.0, 6.0, ((0, 8),), (0, 2, 8, 2.0))
    text_keys = draw_text_keys(jax.random.fold_in(jax.random.fold_in(splits[9], part), 71), part)
    text_values = scatter_about(part_keys[7], (TEXT, D), 1.0, 6.0)
    text_length = jax.random.randint(part_keys[8], (1,), TEXT // 2, TEXT + 1).astype(jnp.int32)
    return {"temporal_queries": temporal_queries, "temporal_keys": temporal_keys, "temporal_values": temporal_values, "temporal_cotangent": temporal_cotangent, "cross_queries": cross_queries, "cross_cotangent": cross_cotangent, "text_keys": text_keys, "text_values": text_values, "text_length": text_length}


def attend_back(queries, targets, values, cotangent, keep, scale):
    highest = lax.Precision.HIGHEST
    query_f = queries.astype(jnp.float32)
    target_f = targets.astype(jnp.float32)
    value_f = values.astype(jnp.float32)
    cotan_f = cotangent.astype(jnp.float32)
    scores = jnp.einsum('mhe,nhe->hmn', query_f, target_f, precision=highest) * scale
    if keep is not None:
        scores = jnp.where(keep, scores, -1e+30)
    highest_score = lax.optimization_barrier(jnp.max(scores, axis=-1, keepdims=True))
    expo = jnp.exp(scores - highest_score)
    weights = expo / lax.optimization_barrier(jnp.sum(expo, axis=-1, keepdims=True))
    rounded = lax.optimization_barrier(weights.astype(jnp.bfloat16)).astype(jnp.float32)
    output = jnp.einsum('hmn,nhe->mhe', rounded, value_f, precision=highest)
    deltas = lax.optimization_barrier(jnp.sum(cotan_f * output, axis=-1))
    grad_values = jnp.einsum('hmn,mhe->nhe', rounded, cotan_f, precision=highest)
    products = jnp.einsum('mhe,nhe->hmn', cotan_f, value_f, precision=highest)
    slopes = weights * (products - jnp.transpose(deltas)[:, :, None]) * scale
    sloped = lax.optimization_barrier(slopes.astype(jnp.bfloat16)).astype(jnp.float32)
    grad_queries = jnp.einsum('hmn,nhe->mhe', sloped, target_f, precision=highest)
    grad_targets = jnp.einsum('hmn,mhe->nhe', sloped, query_f, precision=highest)
    return (grad_queries, grad_targets, grad_values)

def reference(temporal_queries, temporal_keys, temporal_values, temporal_cotangent, cross_queries, cross_cotangent, text_keys, text_values, text_length):
    scale = 1.0 / math.sqrt(HEAD_DIM)

    def split_heads(array):
        return array.reshape(FRAMES, POS, HEADS, HEAD_DIM).transpose(1, 0, 2, 3)

    def merge_heads(array):
        return array.transpose(1, 0, 2, 3).reshape(FRAMES, POS, D).astype(jnp.bfloat16)

    def one_column(group):
        return attend_back(group[0], group[1], group[2], group[3], None, scale)
    grad_query, grad_key, grad_value = lax.map(one_column, (split_heads(temporal_queries), split_heads(temporal_keys), split_heads(temporal_values), split_heads(temporal_cotangent)))
    keep = (jnp.arange(TEXT, dtype=jnp.int32) < text_length[0].astype(jnp.int32))[None, None, :]
    text_heads = text_keys.reshape(TEXT, HEADS, HEAD_DIM)
    value_heads = text_values.reshape(TEXT, HEADS, HEAD_DIM)

    def one_frame(carry, group):
        frame_query = group[0].reshape(POS, HEADS, HEAD_DIM)
        frame_cotan = group[1].reshape(POS, HEADS, HEAD_DIM)
        grads = attend_back(frame_query, text_heads, value_heads, frame_cotan, keep, scale)
        return ((carry[0] + grads[1], carry[1] + grads[2]), grads[0].reshape(POS, D).astype(jnp.bfloat16))
    zeros = jnp.zeros((TEXT, HEADS, HEAD_DIM), jnp.float32)
    sums, cross_grad = lax.scan(one_frame, (zeros, zeros), (cross_queries, cross_cotangent))
    text_grad = jnp.concatenate([sums[0], sums[1]], axis=2).reshape(TEXT, 2 * D)
    return (merge_heads(grad_query), merge_heads(grad_key), merge_heads(grad_value), cross_grad, text_grad)
```

```python
import math
from functools import partial

import jax
import jax.numpy as jnp
from jax import lax
from jax.experimental import pallas as pl
from jax.experimental.pallas import tpu as pltpu
from jax.sharding import PartitionSpec as P

HEADS = 16
AXIS = "seq"
MOST_DIRECT = 8


VMEM = pl.BlockSpec(memory_space=pltpu.VMEM)
SMEM = pl.BlockSpec(memory_space=pltpu.SMEM)


def dot_last(a, b):
    return lax.dot_general(a, b, (((1,), (1,)), ((), ())), preferred_element_type=jnp.float32)


def dot_first(a, b):
    return lax.dot_general(a, b, (((0,), (0,)), ((), ())), preferred_element_type=jnp.float32)


def attend_back(q, k, v, c, keep, scale):
    scores = jnp.where(keep, dot_last(q, k) * scale, -1e30)
    expo = jnp.exp(scores - jnp.max(scores, axis=-1, keepdims=True))
    weights = expo / jnp.sum(expo, axis=-1, keepdims=True)
    rounded = weights.astype(jnp.bfloat16)
    products = dot_last(c, v)
    delta = jnp.sum(rounded.astype(jnp.float32) * products, axis=-1, keepdims=True)
    sloped = (weights * (products - delta) * scale).astype(jnp.bfloat16)
    grad_q = jnp.dot(sloped, k, preferred_element_type=jnp.float32)
    return grad_q, dot_first(sloped, q), dot_first(rounded, c)


def cross_kernel(n, fold, len_ref, q_ref, c_ref, k_ref, v_ref, grad_ref, stay_ref, send_ref):
    rows, width = q_ref.shape
    text = k_ref.shape[0]
    head_dim = width // HEADS
    scale = 1.0 / math.sqrt(head_dim)
    keep = lax.broadcasted_iota(jnp.int32, (rows, text), 1) < len_ref[0]
    groups = n if fold else 1
    per = HEADS // groups
    me = lax.axis_index(AXIS) if fold else 0
    for g in range(groups):
        parts = []
        for h in range(g * per, (g + 1) * per):
            cols = slice(h * head_dim, (h + 1) * head_dim)
            gq, gk, gv = attend_back(
                q_ref[:, cols], k_ref[:, cols], v_ref[:, cols], c_ref[:, cols], keep, scale
            )
            grad_ref[:, cols] = gq.astype(grad_ref.dtype)
            parts += [gk, gv]
        if not fold:
            for i, part in enumerate(parts):
                stay_ref[:, i * head_dim : (i + 1) * head_dim] = part
            continue
        block = jnp.concatenate(parts, axis=1)
        span = text // fold
        block = jnp.concatenate([block[i * span : (i + 1) * span] for i in range(fold)], axis=1)
        place = me ^ g

        @pl.when(place % 2 == 0)
        def _():
            stay_ref[place // 2] = block

        @pl.when(place % 2 == 1)
        def _():
            send_ref[place // 2] = block.astype(send_ref.dtype)


def temporal_kernel(slots, lanes, *refs):
    ins, outs, buf = refs[:slots], refs[slots : 2 * slots], refs[2 * slots]
    rows, width = buf.shape[1:]
    each = rows // slots
    head_dim = width // HEADS
    scale = 1.0 / math.sqrt(head_dim)
    for i, ref in enumerate(ins):
        for t in range(4):
            buf[t, i * each : (i + 1) * each] = ref[t]
    keep = (
        lax.broadcasted_iota(jnp.int32, (rows, rows), 0) % lanes
        == lax.broadcasted_iota(jnp.int32, (rows, rows), 1) % lanes
    )
    for h in range(HEADS):
        cols = slice(h * head_dim, (h + 1) * head_dim)
        q, k, v, c = (buf[t, :, cols] for t in range(4))
        for t, grad in enumerate(attend_back(q, k, v, c, keep, scale)):
            buf[4 + t, :, cols] = grad.astype(buf.dtype)
    for i, ref in enumerate(outs):
        for t in range(3):
            ref[t] = buf[4 + t, i * each : (i + 1) * each]


def pack_kernel(slots, *refs):
    ins, outs = refs[:4], refs[4:]
    each = ins[0].shape[0] // slots
    me = lax.axis_index(AXIS)
    for k, out in enumerate(outs):
        start = pl.multiple_of((me ^ k) * each, each)
        for t, ref in enumerate(ins):
            out[t] = ref[pl.ds(start, each), :]


def unpack_kernel(slots, fold, *refs):
    ins, (kept, got), outs = refs[:slots], refs[slots : slots + 2], refs[slots + 2 :]
    each = outs[0].shape[0] // slots
    me = lax.axis_index(AXIS)
    for k, ref in enumerate(ins):
        start = pl.multiple_of((me ^ k) * each, each)
        for t in range(3):
            outs[t][pl.ds(start, each), :] = ref[t]
    total = kept[0] + got[0].astype(jnp.float32)
    span, columns = total.shape[0], total.shape[1] // fold
    for i in range(fold):
        outs[3][i * span : (i + 1) * span, :] = total[:, i * columns : (i + 1) * columns]


def cost(flops, moved):
    return pl.CostEstimate(flops=int(flops), bytes_accessed=int(moved), transcendentals=0)


def bf16(*shape):
    return jax.ShapeDtypeStruct(shape, jnp.bfloat16)


def f32(*shape):
    return jax.ShapeDtypeStruct(shape, jnp.float32)


def local(n, tq, tk, tv, tc, cq, cc, text_k, text_v, text_len):
    frames, positions, width = tq.shape
    rows = frames * positions
    text = text_k.shape[0]
    lanes = positions // n
    columns = 2 * width // n
    fold = 128 // math.gcd(columns, 128)
    direct = (
        frames == 1
        and n <= MOST_DIRECT
        and n & (n - 1) == 0
        and HEADS % n == 0
        and positions % (8 * n) == 0
        and text % (8 * fold) == 0
    )
    flat = [x.reshape(rows, width) for x in (tq, tk, tv, tc)]
    big = cost(40 * rows * text * width, 12 * rows * width)

    def swap(x, k):
        return lax.ppermute(x, AXIS, [(i, i ^ k) for i in range(n)])

    def cross(fold, *text_out):
        return pl.pallas_call(
            partial(cross_kernel, n, fold),
            out_shape=(bf16(rows, width),) + text_out,
            in_specs=[SMEM] + [VMEM] * 4,
            out_specs=(VMEM,) * (1 + len(text_out)),
            cost_estimate=big,
            name="cross",
        )

    cross_args = (text_len, cq.reshape(rows, width), cc.reshape(rows, width), text_k, text_v)

    def temporal(messages, each):
        count = len(messages)
        return pl.pallas_call(
            partial(temporal_kernel, count, lanes),
            out_shape=tuple(bf16(3, each, width) for _ in messages),
            in_specs=[VMEM] * count,
            out_specs=(VMEM,) * count,
            scratch_shapes=[pltpu.VMEM((7, rows, width), jnp.bfloat16)],
            cost_estimate=big,
            name="temporal",
        )(*messages)

    if not direct:
        packed = jnp.stack(flat).reshape(4, frames, n, lanes, width).transpose(2, 0, 1, 3, 4)
        moved = lax.all_to_all(packed, AXIS, 0, 0, tiled=True)
        moved = moved.transpose(1, 0, 2, 3, 4).reshape(4, rows, width)
        grad_cross, partials = pl.pallas_call(
            lambda *refs: cross_kernel(n, 0, *refs, None),
            out_shape=(bf16(rows, width), f32(text, 2 * width)),
            in_specs=[SMEM] + [VMEM] * 4,
            out_specs=(VMEM, VMEM),
            cost_estimate=big,
            name="cross",
        )(*cross_args)
        text_grad = lax.psum_scatter(partials, AXIS, scatter_dimension=1, tiled=True)
        (back,) = temporal([moved], rows)
        back = back.reshape(3, n, frames, lanes, width).transpose(1, 0, 2, 3, 4)
        back = lax.all_to_all(back, AXIS, 0, 0, tiled=True)
        back = back.transpose(1, 2, 0, 3, 4).reshape(3, frames, positions, width)
        return back[0], back[1], back[2], grad_cross.reshape(cq.shape), text_grad

    each = positions // n
    messages = pl.pallas_call(
        partial(pack_kernel, n),
        out_shape=tuple(bf16(4, each, width) for _ in range(n)),
        in_specs=[VMEM] * 4,
        out_specs=(VMEM,) * n,
        cost_estimate=cost(0, 16 * rows * width),
        name="pack",
    )(*flat)
    order = sorted(range(1, n), key=lambda k: (-(k.bit_length()), k))
    came = {0: messages[0]}
    for k in order:
        came[k] = swap(messages[k], k)

    span = text // fold
    grad_cross, stay, send = cross(
        fold, f32(n // 2, span, fold * columns), bf16(n // 2, span, fold * columns)
    )(*cross_args)
    step = 1
    while True:
        got = swap(send, step)
        step *= 2
        if step == n:
            break
        both = stay + got.astype(jnp.float32)
        both = both.reshape(-1, 2, span, fold * columns)
        stay, send = both[:, 0], both[:, 1].astype(jnp.bfloat16)

    back = temporal([came[k] for k in range(n)], each)
    home = {0: back[0]}
    for k in order:
        home[k] = swap(back[k], k)
    out = pl.pallas_call(
        partial(unpack_kernel, n, fold),
        out_shape=(bf16(rows, width),) * 3 + (f32(text, columns),),
        in_specs=[VMEM] * (n + 2),
        out_specs=(VMEM,) * 4,
        cost_estimate=cost(0, 12 * rows * width),
        name="unpack",
    )(*[home[k] for k in range(n)], stay, got)
    return tuple(x.reshape(tq.shape) for x in out[:3]) + (grad_cross.reshape(cq.shape), out[3])


def solution(mesh):
    token = P(("clip", "seq"), None, None)
    return jax.shard_map(
        partial(local, mesh.shape[AXIS]),
        mesh=mesh,
        in_specs=(token,) * 6 + (P("clip", None), P("clip", None), P("clip")),
        out_specs=(token,) * 4 + (P("clip", "seq"),),
        check_vma=False,
    )
```

```python
import math
from functools import partial

import jax
import jax.numpy as jnp
from jax import lax
from jax.experimental import pallas as pl
from jax.experimental.pallas import tpu as pltpu
from jax.sharding import PartitionSpec as P

HEADS = 16
AXIS = "seq"
MOST_DIRECT = 8


VMEM = pl.BlockSpec(memory_space=pltpu.VMEM)
HBM = pl.BlockSpec(memory_space=pltpu.HBM)
SMEM = pl.BlockSpec(memory_space=pltpu.SMEM)


def dot_last(a, b):
    return lax.dot_general(a, b, (((1,), (1,)), ((), ())), preferred_element_type=jnp.float32)


def dot_first(a, b):
    return lax.dot_general(a, b, (((0,), (0,)), ((), ())), preferred_element_type=jnp.float32)


def attend_back(q, k, v, c, keep, scale):
    scores = jnp.where(keep, dot_last(k, q), -1e30)
    expo = jnp.exp((scores - jnp.max(scores, axis=0, keepdims=True)) * scale)
    weights = expo * (1.0 / jnp.sum(expo, axis=0, keepdims=True))
    rounded = weights.astype(jnp.bfloat16)
    products = dot_last(v, c)
    delta = jnp.sum(rounded.astype(jnp.float32) * products, axis=0, keepdims=True)
    sloped = (weights * (products - delta) * scale).astype(jnp.bfloat16)
    return (
        dot_first(sloped, k),
        jnp.dot(sloped, q, preferred_element_type=jnp.float32),
        jnp.dot(rounded, c, preferred_element_type=jnp.float32),
    )


def cross_kernel(n, fold, len_ref, q_ref, c_ref, k_ref, v_ref, grad_ref, stay_ref, send_ref):
    rows, width = q_ref.shape
    text = k_ref.shape[0]
    head_dim = width // HEADS
    scale = 1.0 / math.sqrt(head_dim)
    keep = lax.broadcasted_iota(jnp.int32, (text, rows), 0) < len_ref[0]
    groups = n if fold else 1
    per = HEADS // groups
    me = lax.axis_index(AXIS) if fold else 0
    for g in range(groups):
        parts = []
        for h in range(g * per, (g + 1) * per):
            cols = slice(h * head_dim, (h + 1) * head_dim)
            gq, gk, gv = attend_back(
                q_ref[:, cols], k_ref[:, cols], v_ref[:, cols], c_ref[:, cols], keep, scale
            )
            grad_ref[:, cols] = gq.astype(grad_ref.dtype)
            parts += [gk, gv]
        if not fold:
            for i, part in enumerate(parts):
                stay_ref[:, i * head_dim : (i + 1) * head_dim] = part
            continue
        block = jnp.concatenate(parts, axis=1)
        span = text // fold
        block = jnp.concatenate([block[i * span : (i + 1) * span] for i in range(fold)], axis=1)
        place = me ^ g

        @pl.when(place % 2 == 0)
        def _():
            stay_ref[place // 2] = block

        @pl.when(place % 2 == 1)
        def _():
            send_ref[place // 2] = block.astype(send_ref.dtype)


def temporal_kernel(slots, lanes, *refs):
    ins, outs = refs[:slots], refs[slots:]
    each, width = ins[0].shape[1:]
    rows = each * slots
    head_dim = width // HEADS
    scale = 1.0 / math.sqrt(head_dim)
    keep = (
        lax.broadcasted_iota(jnp.int32, (rows, rows), 0) % lanes
        == lax.broadcasted_iota(jnp.int32, (rows, rows), 1) % lanes
    )
    whole = [jnp.concatenate([ref[t] for ref in ins], axis=0) for t in range(4)]
    for h in range(HEADS):
        cols = slice(h * head_dim, (h + 1) * head_dim)
        q, k, v, c = (x[:, cols] for x in whole)
        for t, grad in enumerate(attend_back(q, k, v, c, keep, scale)):
            grad = grad.astype(jnp.bfloat16)
            for i, ref in enumerate(outs):
                ref[t, :, cols] = grad[i * each : (i + 1) * each]


def pack_kernel(slots, *refs):
    ins, outs, sems = refs[:4], refs[4:-1], refs[-1]
    each = ins[0].shape[0] // slots
    me = lax.axis_index(AXIS)
    copies = []
    for k, out in enumerate(outs):
        start = pl.multiple_of((me ^ k) * each, each)
        for t, ref in enumerate(ins):
            copies.append(
                pltpu.make_async_copy(ref.at[pl.ds(start, each)], out.at[t], sems.at[k, t])
            )
    for copy in copies:
        copy.start()
    for copy in copies:
        copy.wait()


def unpack_kernel(slots, fold, *refs):
    ins, (kept, got), outs = refs[:slots], refs[slots : slots + 2], refs[slots + 2 :]
    each = outs[0].shape[0] // slots
    me = lax.axis_index(AXIS)
    for k, ref in enumerate(ins):
        start = pl.multiple_of((me ^ k) * each, each)
        for t in range(3):
            outs[t][pl.ds(start, each), :] = ref[t]
    total = kept[0] + got[0].astype(jnp.float32)
    span, columns = total.shape[0], total.shape[1] // fold
    for i in range(fold):
        outs[3][i * span : (i + 1) * span, :] = total[:, i * columns : (i + 1) * columns]


PARAMS = pltpu.CompilerParams(vmem_limit_bytes=16 << 20)


def cost(flops, moved):
    return pl.CostEstimate(flops=int(flops), bytes_accessed=int(moved), transcendentals=0)


def bf16(*shape):
    return jax.ShapeDtypeStruct(shape, jnp.bfloat16)


def f32(*shape):
    return jax.ShapeDtypeStruct(shape, jnp.float32)


def local(n, tq, tk, tv, tc, cq, cc, text_k, text_v, text_len):
    frames, positions, width = tq.shape
    rows = frames * positions
    text = text_k.shape[0]
    lanes = positions // n
    columns = 2 * width // n
    fold = 128 // math.gcd(columns, 128)
    direct = (
        frames == 1
        and n <= MOST_DIRECT
        and n & (n - 1) == 0
        and HEADS % n == 0
        and positions % (8 * n) == 0
        and text % (8 * fold) == 0
    )
    flat = [x.reshape(rows, width) for x in (tq, tk, tv, tc)]
    big = cost(40 * rows * text * width, 12 * rows * width)

    def swap(x, k):
        return lax.ppermute(x, AXIS, [(i, i ^ k) for i in range(n)])

    def cross(fold, *text_out):
        return pl.pallas_call(
            partial(cross_kernel, n, fold),
            out_shape=(bf16(rows, width),) + text_out,
            in_specs=[SMEM] + [VMEM] * 4,
            out_specs=(VMEM,) * (1 + len(text_out)),
            cost_estimate=big,
            compiler_params=PARAMS,
            name="cross",
        )

    cross_args = (text_len, cq.reshape(rows, width), cc.reshape(rows, width), text_k, text_v)

    def temporal(messages, each):
        count = len(messages)
        return pl.pallas_call(
            partial(temporal_kernel, count, lanes),
            out_shape=tuple(bf16(3, each, width) for _ in messages),
            in_specs=[VMEM] * count,
            out_specs=(VMEM,) * count,
            cost_estimate=big,
            compiler_params=PARAMS,
            name="temporal",
        )(*messages)

    if not direct:
        packed = jnp.stack(flat).reshape(4, frames, n, lanes, width).transpose(2, 0, 1, 3, 4)
        moved = lax.all_to_all(packed, AXIS, 0, 0, tiled=True)
        moved = moved.transpose(1, 0, 2, 3, 4).reshape(4, rows, width)
        grad_cross, partials = pl.pallas_call(
            lambda *refs: cross_kernel(n, 0, *refs, None),
            out_shape=(bf16(rows, width), f32(text, 2 * width)),
            in_specs=[SMEM] + [VMEM] * 4,
            out_specs=(VMEM, VMEM),
            cost_estimate=big,
            compiler_params=PARAMS,
            name="cross",
        )(*cross_args)
        text_grad = lax.psum_scatter(partials, AXIS, scatter_dimension=1, tiled=True)
        (back,) = temporal([moved], rows)
        back = back.reshape(3, n, frames, lanes, width).transpose(1, 0, 2, 3, 4)
        back = lax.all_to_all(back, AXIS, 0, 0, tiled=True)
        back = back.transpose(1, 2, 0, 3, 4).reshape(3, frames, positions, width)
        return back[0], back[1], back[2], grad_cross.reshape(cq.shape), text_grad

    each = positions // n
    messages = pl.pallas_call(
        partial(pack_kernel, n),
        out_shape=tuple(bf16(4, each, width) for _ in range(n)),
        in_specs=[HBM] * 4,
        out_specs=(VMEM,) * n,
        scratch_shapes=[pltpu.SemaphoreType.DMA((n, 4))],
        cost_estimate=cost(0, 16 * rows * width),
        compiler_params=PARAMS,
        name="pack",
    )(*[pltpu.with_memory_space_constraint(x, pltpu.HBM) for x in flat])
    messages, cross_args = lax.optimization_barrier((messages, cross_args))
    order = sorted(range(1, n), key=lambda k: (-(k.bit_length()), k))
    came = {0: messages[0]}
    for k in order:
        came[k] = swap(messages[k], k)

    span = text // fold
    grad_cross, stay, send = cross(
        fold, f32(n // 2, span, fold * columns), bf16(n // 2, span, fold * columns)
    )(*cross_args)
    step = 1
    while True:
        got = swap(send, step)
        step *= 2
        if step == n:
            break
        both = stay + got.astype(jnp.float32)
        both = both.reshape(-1, 2, span, fold * columns)
        stay, send = both[:, 0], both[:, 1].astype(jnp.bfloat16)

    back = temporal([came[k] for k in range(n)], each)
    home = {0: back[0]}
    for k in order:
        home[k] = swap(back[k], k)
    out = pl.pallas_call(
        partial(unpack_kernel, n, fold),
        out_shape=(bf16(rows, width),) * 3 + (f32(text, columns),),
        in_specs=[VMEM] * (n + 2),
        out_specs=(VMEM,) * 4,
        cost_estimate=cost(0, 12 * rows * width),
        compiler_params=PARAMS,
        name="unpack",
    )(*[home[k] for k in range(n)], stay, got)
    return tuple(x.reshape(tq.shape) for x in out[:3]) + (grad_cross.reshape(cq.shape), out[3])


def solution(mesh):
    n = mesh.shape[AXIS]
    token = P(("clip", "seq"), None, None)

    def body(*args):
        return local(n, *args)

    step = jax.shard_map(
        body,
        mesh=mesh,
        in_specs=(token,) * 6 + (P("clip", None), P("clip", None), P("clip")),
        out_specs=(token,) * 4 + (P("clip", "seq"),),
        check_vma=False,
    )
    return step if 4 <= n <= MOST_DIRECT else step
```

```python
import math
from functools import partial

import jax
import jax.numpy as jnp
from jax import lax
from jax.experimental import pallas as pl
from jax.experimental.pallas import tpu as pltpu
from jax.sharding import PartitionSpec as P

HEADS = 16
LANES = 128
AXIS = "seq"
MOST_DIRECT = 8


VMEM = pl.BlockSpec(memory_space=pltpu.VMEM)
HBM = pl.BlockSpec(memory_space=pltpu.HBM)
SMEM = pl.BlockSpec(memory_space=pltpu.SMEM)


def dot(a, b, along_a, along_b):
    dims = (((along_a,), (along_b,)), ((), ()))
    return lax.dot_general(a, b, dims, preferred_element_type=jnp.float32)


class Heads:
    def __init__(self, width):
        self.size = width // HEADS
        self.tiles = width // LANES
        self.masks = {}

    def mask(self, low, high):
        if (low, high) not in self.masks:
            lane = lax.broadcasted_iota(jnp.int32, (1, LANES), 1)
            inside = ((lane >= low) & (lane < high)).astype(jnp.float32)
            self.masks[low, high] = inside.astype(jnp.bfloat16)
        return self.masks[low, high]

    def touched(self, head):
        return range(head * self.size // LANES, -(-(head + 1) * self.size // LANES))

    def tile(self, x, t):
        return x[:, t * LANES : (t + 1) * LANES]

    def only(self, x, head, t):
        low = max(head * self.size - t * LANES, 0)
        high = min((head + 1) * self.size - t * LANES, LANES)
        return self.tile(x, t) * self.mask(low, high)

    def placed(self, x, head, to):
        start, out = head * self.size, {}
        for t in self.touched(head):
            turn = (to - start) % LANES
            turned = pltpu.roll(self.tile(x, t), turn, 1) if turn else self.tile(x, t)
            for u in range(to // LANES, -(-(to + self.size) // LANES)):
                low = max(0, LANES * t - start, LANES * u - to)
                high = min(self.size, LANES * (t + 1) - start, LANES * (u + 1) - to)
                if low < high:
                    part = turned * self.mask(to + low - LANES * u, to + high - LANES * u)
                    out[u] = out[u] + part if u in out else part
        return out

    def products(self, q, k, v, c, head):
        tiles = self.touched(head)
        ks = {t: self.only(k, head, t) for t in tiles}
        cs = {t: self.only(c, head, t) for t in tiles}
        scores = dot(beside(ks.values()), beside([self.tile(q, t) for t in tiles]), 1, 1)
        products = dot(beside([self.tile(v, t) for t in tiles]), beside(cs.values()), 1, 1)
        return scores, products, ks, cs


def beside(parts):
    parts = list(parts)
    return parts[0] if len(parts) == 1 else jnp.concatenate(parts, axis=1)


def below(parts):
    parts = list(parts)
    return parts[0] if len(parts) == 1 else jnp.concatenate(parts, axis=0)


def softmax_back(scores, products, keep, scale):
    scores = jnp.where(keep, scores, -1e30)
    expo = jnp.exp((scores - jnp.max(scores, axis=0, keepdims=True)) * scale)
    weights = expo * (1.0 / jnp.sum(expo, axis=0, keepdims=True))
    rounded = weights.astype(jnp.bfloat16)
    delta = jnp.sum(rounded.astype(jnp.float32) * products, axis=0, keepdims=True)
    return rounded, (weights * (products - delta) * scale).astype(jnp.bfloat16)


def attend_back(heads, q, k, v, c, keep, ahead, each_head, each_tile):
    scale = 1.0 / math.sqrt(heads.size)
    first, ready, tile = {}, {}, 0
    for step in range(HEADS + ahead):
        if step < HEADS:
            first[step] = heads.products(q, k, v, c, step)
        h = step - ahead
        if h < 0:
            continue
        scores, products, ks, cs = first.pop(h)
        rounded, sloped = softmax_back(scores, products, keep, scale)
        ready[h] = (rounded, sloped, ks, cs)
        each_head(h, rounded, sloped)
        while tile < heads.tiles and (tile + 1) * LANES <= (h + 1) * heads.size:
            parts = [
                (g, r, s, ks[tile], cs[tile])
                for g, (r, s, ks, cs) in sorted(ready.items())
                if tile in heads.touched(g)
            ]
            each_tile(tile, parts)
            ready = {g: x for g, x in ready.items() if heads.touched(g)[-1] > tile}
            tile += 1


def cross_kernel(groups, len_ref, q_ref, c_ref, k_ref, v_ref, grad_ref, *text_refs):
    rows, width = q_ref.shape
    text = k_ref.shape[0]
    heads = Heads(width)
    keep = lax.broadcasted_iota(jnp.int32, (text, rows), 0) < len_ref[0]
    q, c, k, v = q_ref[...], c_ref[...], k_ref[...], v_ref[...]
    per = HEADS // groups
    rest = 2 * per * heads.size % LANES
    terms, blocks = {}, []
    me = lax.axis_index(AXIS) if groups > 1 else 0

    def each_head(h, rounded, sloped):
        block, i = divmod(h, per)
        for left, x, to in ((sloped, q, 2 * i), (rounded, c, 2 * i + 1)):
            for t, value in heads.placed(x, h, to * heads.size).items():
                terms.setdefault(t, []).append((left, value))
        if i < per - 1:
            return
        tiles = [dot(beside(a for a, _ in x), below(b for _, b in x), 1, 0) for x in terms.values()]
        terms.clear()
        if rest:
            last, span = tiles.pop(), text * rest // LANES
            tiles.append(
                sum(
                    pltpu.roll(last[i * span : (i + 1) * span], i * rest, 1)
                    if i
                    else last[:span]
                    for i in range(LANES // rest)
                )
            )
        blocks.append(below(tiles))
        if groups == 1:
            text_refs[0][0] = blocks.pop()
        elif block % 2:
            odd, even = blocks.pop(), blocks.pop()
            place = (block // 2) ^ (me // 2)
            swapped = me % 2 == 1
            text_refs[0][place] = jnp.where(swapped, odd, even)
            text_refs[1][place] = jnp.where(swapped, even, odd).astype(jnp.bfloat16)

    def each_tile(t, parts):
        grad = dot(below(s for _, _, s, _, _ in parts), below(k for *_, k, _ in parts), 0, 0)
        grad_ref[:, t * LANES : (t + 1) * LANES] = grad.astype(jnp.bfloat16)

    attend_back(heads, q, k, v, c, keep, 6, each_head, each_tile)


def temporal_kernel(slots, lanes, *refs):
    ins, outs = refs[:slots], refs[slots:]
    each, width = ins[0].shape[1:]
    rows = each * slots
    heads = Heads(width)
    keep = (
        lax.broadcasted_iota(jnp.int32, (rows, rows), 0) % lanes
        == lax.broadcasted_iota(jnp.int32, (rows, rows), 1) % lanes
    )
    q, k, v, c = (below(ref[t] for ref in ins) for t in range(4))

    def each_tile(t, parts):
        slopes = [s for _, _, s, _, _ in parts]
        grads = (
            dot(below(slopes), below(k for *_, k, _ in parts), 0, 0),
            dot(beside(slopes), below(heads.only(q, g, t) for g, *_ in parts), 1, 0),
            dot(beside(r for _, r, *_ in parts), below(c for *_, c in parts), 1, 0),
        )
        for x, grad in enumerate(grads):
            grad = grad.astype(jnp.bfloat16)
            for i, ref in enumerate(outs):
                ref[x, :, t * LANES : (t + 1) * LANES] = grad[i * each : (i + 1) * each]

    attend_back(heads, q, k, v, c, keep, 8, lambda *_: None, each_tile)


def pack_kernel(slots, *refs):
    ins, outs, sems = refs[:4], refs[4:-1], refs[-1]
    each = ins[0].shape[0] // slots
    me = lax.axis_index(AXIS)
    copies = []
    for k, out in enumerate(outs):
        start = pl.multiple_of((me ^ k) * each, each)
        for t, ref in enumerate(ins):
            copies.append(
                pltpu.make_async_copy(ref.at[pl.ds(start, each)], out.at[t], sems.at[k, t])
            )
    for copy in copies:
        copy.start()
    for copy in copies:
        copy.wait()


def unpack_kernel(slots, *refs):
    ins, (kept, got), outs = refs[:slots], refs[slots : slots + 2], refs[slots + 2 :]
    each = outs[0].shape[0] // slots
    me = lax.axis_index(AXIS)
    for k, ref in enumerate(ins):
        start = pl.multiple_of((me ^ k) * each, each)
        for t in range(3):
            outs[t][pl.ds(start, each), :] = ref[t]
    total = kept[0] + got[0].astype(jnp.float32)
    text, columns = outs[3].shape
    whole, rest = divmod(columns, LANES)
    for t in range(whole):
        outs[3][:, t * LANES : (t + 1) * LANES] = total[t * text : (t + 1) * text]
    span = text * rest // LANES
    for i in range(LANES // rest if rest else 0):
        last = total[whole * text : whole * text + span, i * rest : (i + 1) * rest]
        outs[3][i * span : (i + 1) * span, whole * LANES :] = last


PARAMS = pltpu.CompilerParams(vmem_limit_bytes=16 << 20)


def cost(flops, moved):
    return pl.CostEstimate(flops=int(flops), bytes_accessed=int(moved), transcendentals=0)


def bf16(*shape):
    return jax.ShapeDtypeStruct(shape, jnp.bfloat16)


def f32(*shape):
    return jax.ShapeDtypeStruct(shape, jnp.float32)


def local(n, tq, tk, tv, tc, cq, cc, text_k, text_v, text_len):
    frames, positions, width = tq.shape
    rows = frames * positions
    text = text_k.shape[0]
    lanes = positions // n
    columns = 2 * width // n
    rest = columns % LANES
    direct = (
        frames == 1
        and 4 <= n <= MOST_DIRECT
        and n & (n - 1) == 0
        and HEADS % n == 0
        and positions % (8 * n) == 0
        and (rest == 0 or (LANES % rest == 0 and text * rest % (8 * LANES) == 0))
    )
    flat = [x.reshape(rows, width) for x in (tq, tk, tv, tc)]
    big = cost(40 * rows * text * width, 12 * rows * width)

    def swap(x, k):
        return lax.ppermute(x, AXIS, [(i, i ^ k) for i in range(n)])

    def cross(groups, *text_out):
        return pl.pallas_call(
            partial(cross_kernel, groups),
            out_shape=(bf16(rows, width),) + text_out,
            in_specs=[SMEM] + [VMEM] * 4,
            out_specs=(VMEM,) * (1 + len(text_out)),
            cost_estimate=big,
            compiler_params=PARAMS,
            name="cross",
        )(*cross_args)

    cross_args = (text_len, cq.reshape(rows, width), cc.reshape(rows, width), text_k, text_v)

    def temporal(messages, each):
        count = len(messages)
        return pl.pallas_call(
            partial(temporal_kernel, count, lanes),
            out_shape=tuple(bf16(3, each, width) for _ in messages),
            in_specs=[VMEM] * count,
            out_specs=(VMEM,) * count,
            cost_estimate=big,
            compiler_params=PARAMS,
            name="temporal",
        )(*messages)

    if not direct:
        packed = jnp.stack(flat).reshape(4, frames, n, lanes, width).transpose(2, 0, 1, 3, 4)
        moved = lax.all_to_all(packed, AXIS, 0, 0, tiled=True)
        moved = moved.transpose(1, 0, 2, 3, 4).reshape(4, rows, width)
        tiles = 2 * width // LANES
        grad_cross, partials = cross(1, f32(1, tiles * text, LANES))
        partials = partials.reshape(tiles, text, LANES).transpose(1, 0, 2).reshape(text, -1)
        text_grad = lax.psum_scatter(partials, AXIS, scatter_dimension=1, tiled=True)
        (back,) = temporal([moved], rows)
        back = back.reshape(3, n, frames, lanes, width).transpose(1, 0, 2, 3, 4)
        back = lax.all_to_all(back, AXIS, 0, 0, tiled=True)
        back = back.transpose(1, 2, 0, 3, 4).reshape(3, frames, positions, width)
        return back[0], back[1], back[2], grad_cross.reshape(cq.shape), text_grad

    each = positions // n
    messages = pl.pallas_call(
        partial(pack_kernel, n),
        out_shape=tuple(bf16(4, each, width) for _ in range(n)),
        in_specs=[HBM] * 4,
        out_specs=(VMEM,) * n,
        scratch_shapes=[pltpu.SemaphoreType.DMA((n, 4))],
        cost_estimate=cost(0, 16 * rows * width),
        compiler_params=PARAMS,
        name="pack",
    )(*[pltpu.with_memory_space_constraint(x, pltpu.HBM) for x in flat])
    messages, cross_args = lax.optimization_barrier((messages, cross_args))
    order = sorted(range(1, n), key=lambda k: (-(k.bit_length()), k))
    came = {0: messages[0]}
    for k in order:
        came[k] = swap(messages[k], k)

    high = text * columns // LANES
    grad_cross, stay, send = cross(n, f32(n // 2, high, LANES), bf16(n // 2, high, LANES))
    step = 1
    while True:
        got = swap(send, step)
        step *= 2
        if step == n:
            break
        both = stay + got.astype(jnp.float32)
        both = both.reshape(-1, 2, high, LANES)
        stay, send = both[:, 0], both[:, 1].astype(jnp.bfloat16)

    back = temporal([came[k] for k in range(n)], each)
    home = {0: back[0]}
    for k in order:
        home[k] = swap(back[k], k)
    out = pl.pallas_call(
        partial(unpack_kernel, n),
        out_shape=(bf16(rows, width),) * 3 + (f32(text, columns),),
        in_specs=[VMEM] * (n + 2),
        out_specs=(VMEM,) * 4,
        cost_estimate=cost(0, 12 * rows * width),
        compiler_params=PARAMS,
        name="unpack",
    )(*[home[k] for k in range(n)], stay, got)
    return tuple(x.reshape(tq.shape) for x in out[:3]) + (grad_cross.reshape(cq.shape), out[3])


def solution(mesh):
    n = mesh.shape[AXIS]
    token = P(("clip", "seq"), None, None)

    def body(*args):
        return local(n, *args)

    step = jax.shard_map(
        body,
        mesh=mesh,
        in_specs=(token,) * 6 + (P("clip", None), P("clip", None), P("clip")),
        out_specs=(token,) * 4 + (P("clip", "seq"),),
        check_vma=False,
    )
    return step if 4 <= n <= MOST_DIRECT else step
```

```python
import math
from functools import partial

import jax
import jax.numpy as jnp
from jax import lax
from jax.experimental import pallas as pl
from jax.experimental.pallas import tpu as pltpu
from jax.sharding import PartitionSpec as P

HEADS = 16
LANES = 128
AXIS = "seq"
MOST_DIRECT = 8

CHUNKS = 2


VMEM = pl.BlockSpec(memory_space=pltpu.VMEM)
HBM = pl.BlockSpec(memory_space=pltpu.HBM)
SMEM = pl.BlockSpec(memory_space=pltpu.SMEM)


def dot(a, b, along_a, along_b):
    dims = (((along_a,), (along_b,)), ((), ()))
    return lax.dot_general(a, b, dims, preferred_element_type=jnp.float32)


class Heads:
    def __init__(self, width):
        self.size = width // HEADS
        self.tiles = width // LANES
        self.masks = {}

    def mask(self, low, high):
        if (low, high) not in self.masks:
            lane = lax.broadcasted_iota(jnp.int32, (1, LANES), 1)
            inside = ((lane >= low) & (lane < high)).astype(jnp.float32)
            self.masks[low, high] = inside.astype(jnp.bfloat16)
        return self.masks[low, high]

    def touched(self, head):
        return range(head * self.size // LANES, -(-(head + 1) * self.size // LANES))

    def tile(self, x, t):
        return x[:, t * LANES : (t + 1) * LANES]

    def only(self, x, head, t):
        low = max(head * self.size - t * LANES, 0)
        high = min((head + 1) * self.size - t * LANES, LANES)
        return self.tile(x, t) * self.mask(low, high)

    def placed(self, x, head, to):
        start, out = head * self.size, {}
        for t in self.touched(head):
            turn = (to - start) % LANES
            turned = pltpu.roll(self.tile(x, t), turn, 1) if turn else self.tile(x, t)
            for u in range(to // LANES, -(-(to + self.size) // LANES)):
                low = max(0, LANES * t - start, LANES * u - to)
                high = min(self.size, LANES * (t + 1) - start, LANES * (u + 1) - to)
                if low < high:
                    part = turned * self.mask(to + low - LANES * u, to + high - LANES * u)
                    out[u] = out[u] + part if u in out else part
        return out

    def products(self, q, k, v, c, head):
        tiles = self.touched(head)
        ks = {t: self.only(k, head, t) for t in tiles}
        cs = {t: self.only(c, head, t) for t in tiles}
        scores = dot(beside(ks.values()), beside([self.tile(q, t) for t in tiles]), 1, 1)
        products = dot(beside([self.tile(v, t) for t in tiles]), beside(cs.values()), 1, 1)
        return scores, products, ks, cs


def beside(parts):
    parts = list(parts)
    return parts[0] if len(parts) == 1 else jnp.concatenate(parts, axis=1)


def below(parts):
    parts = list(parts)
    return parts[0] if len(parts) == 1 else jnp.concatenate(parts, axis=0)


def softmax_back(scores, products, keep, scale):
    scores = jnp.where(keep, scores, -1e30)
    expo = jnp.exp((scores - jnp.max(scores, axis=0, keepdims=True)) * scale)
    weights = expo * (1.0 / jnp.sum(expo, axis=0, keepdims=True))
    rounded = weights.astype(jnp.bfloat16)
    delta = jnp.sum(rounded.astype(jnp.float32) * products, axis=0, keepdims=True)
    return rounded, (weights * (products - delta) * scale).astype(jnp.bfloat16)


def attend_back(heads, q, k, v, c, keep, ahead, each_head, each_tile):
    scale = 1.0 / math.sqrt(heads.size)
    first, ready, tile = {}, {}, 0
    for step in range(HEADS + ahead):
        if step < HEADS:
            first[step] = heads.products(q, k, v, c, step)
        h = step - ahead
        if h < 0:
            continue
        scores, products, ks, cs = first.pop(h)
        rounded, sloped = softmax_back(scores, products, keep, scale)
        ready[h] = (rounded, sloped, ks, cs)
        each_head(h, rounded, sloped)
        while tile < heads.tiles and (tile + 1) * LANES <= (h + 1) * heads.size:
            parts = [
                (g, r, s, ks[tile], cs[tile])
                for g, (r, s, ks, cs) in sorted(ready.items())
                if tile in heads.touched(g)
            ]
            each_tile(tile, parts)
            ready = {g: x for g, x in ready.items() if heads.touched(g)[-1] > tile}
            tile += 1


def cross_kernel(groups, len_ref, q_ref, c_ref, k_ref, v_ref, grad_ref, *text_refs):
    rows, width = q_ref.shape
    text = k_ref.shape[0]
    heads = Heads(width)
    keep = lax.broadcasted_iota(jnp.int32, (text, rows), 0) < len_ref[0]
    q, c, k, v = q_ref[...], c_ref[...], k_ref[...], v_ref[...]
    per = HEADS // groups
    rest = 2 * per * heads.size % LANES
    terms, blocks = {}, []
    me = lax.axis_index(AXIS) if groups > 1 else 0

    def each_head(h, rounded, sloped):
        block, i = divmod(h, per)
        for left, x, to in ((sloped, q, 2 * i), (rounded, c, 2 * i + 1)):
            for t, value in heads.placed(x, h, to * heads.size).items():
                terms.setdefault(t, []).append((left, value))
        if i < per - 1:
            return
        tiles = [dot(beside(a for a, _ in x), below(b for _, b in x), 1, 0) for x in terms.values()]
        terms.clear()
        if rest:
            last, span = tiles.pop(), text * rest // LANES
            tiles.append(
                sum(
                    pltpu.roll(last[i * span : (i + 1) * span], i * rest, 1)
                    if i
                    else last[:span]
                    for i in range(LANES // rest)
                )
            )
        blocks.append(below(tiles))
        if groups == 1:
            text_refs[0][0] = blocks.pop()
        elif block % 2:
            odd, even = blocks.pop(), blocks.pop()
            place = (block // 2) ^ (me // 2)
            swapped = me % 2 == 1
            text_refs[0][place] = jnp.where(swapped, odd, even)
            text_refs[1][place] = jnp.where(swapped, even, odd).astype(jnp.bfloat16)

    def each_tile(t, parts):
        grad = dot(below(s for _, _, s, _, _ in parts), below(k for *_, k, _ in parts), 0, 0)
        grad_ref[:, t * LANES : (t + 1) * LANES] = grad.astype(jnp.bfloat16)

    attend_back(heads, q, k, v, c, keep, 6, each_head, each_tile)


def temporal_kernel(slots, chunk, part, period, *refs):
    ins, outs = refs[:slots], refs[-slots:]
    before = refs[slots:-slots]
    width = ins[0].shape[2]
    rows = part * slots
    heads = Heads(width)
    keep = (
        lax.broadcasted_iota(jnp.int32, (rows, rows), 0) % period
        == lax.broadcasted_iota(jnp.int32, (rows, rows), 1) % period
    )

    def mine(ref):
        return slice(None) if ref.shape[1] == part else slice(chunk * part, (chunk + 1) * part)

    q, k, v, c = (below(ref[t, mine(ref)] for ref in ins) for t in range(4))

    def product(left, right):
        if rows % LANES == 0:
            return dot(beside(left), below(right), 1, 0)
        return sum(dot(x, y, 1, 0) for x, y in zip(left, right))

    def each_tile(t, parts):
        slopes = [s for _, _, s, _, _ in parts]
        grads = (
            dot(below(slopes), below(k for *_, k, _ in parts), 0, 0),
            product(slopes, [heads.only(q, g, t) for g, *_ in parts]),
            product([r for _, r, *_ in parts], [c for *_, c in parts]),
        )
        for x, grad in enumerate(grads):
            grad = grad.astype(jnp.bfloat16)
            for i, ref in enumerate(outs):
                ref[x, mine(ref), t * LANES : (t + 1) * LANES] = grad[i * part : (i + 1) * part]

    whole = [ref for ref in outs if ref.shape[1] > part]
    for i, ref in enumerate(before):
        j, place = divmod(i, len(whole))
        whole[place][:, j * part : (j + 1) * part] = ref[...]
    attend_back(heads, q, k, v, c, keep, 8, lambda *_: None, each_tile)


def pack_kernel(each, plan, *refs):
    ins, outs, sems = refs[:4], refs[4:-1], refs[-1]
    me = lax.axis_index(AXIS)
    copies = []
    for i, ((k, first, rows), out) in enumerate(zip(plan, outs)):
        start = pl.multiple_of((me ^ k) * each + first, 8)
        for t, ref in enumerate(ins):
            copies.append(
                pltpu.make_async_copy(ref.at[pl.ds(start, rows)], out.at[t], sems.at[i, t])
            )
    for copy in copies:
        copy.start()
    for copy in copies:
        copy.wait()


def unpack_kernel(each, plan, *refs):
    count = len(plan)
    ins, (kept, got), outs = refs[:count], refs[count : count + 2], refs[count + 2 :]
    me = lax.axis_index(AXIS)
    for (k, first, rows), ref in zip(plan, ins):
        start = pl.multiple_of((me ^ k) * each + first, 8)
        for t in range(3):
            outs[t][pl.ds(start, rows), :] = ref[t]
    total = kept[0] + got[0].astype(jnp.float32)
    text, columns = outs[3].shape
    whole, rest = divmod(columns, LANES)
    for t in range(whole):
        outs[3][:, t * LANES : (t + 1) * LANES] = total[t * text : (t + 1) * text]
    span = text * rest // LANES
    for i in range(LANES // rest if rest else 0):
        last = total[whole * text : whole * text + span, i * rest : (i + 1) * rest]
        outs[3][i * span : (i + 1) * span, whole * LANES :] = last


PARAMS = pltpu.CompilerParams(vmem_limit_bytes=16 << 20)


def cost(flops, moved):
    return pl.CostEstimate(flops=int(flops), bytes_accessed=int(moved), transcendentals=0)


def bf16(*shape):
    return jax.ShapeDtypeStruct(shape, jnp.bfloat16)


def f32(*shape):
    return jax.ShapeDtypeStruct(shape, jnp.float32)


def local(n, tq, tk, tv, tc, cq, cc, text_k, text_v, text_len):
    frames, positions, width = tq.shape
    rows = frames * positions
    text = text_k.shape[0]
    lanes = positions // n
    columns = 2 * width // n
    rest = columns % LANES
    direct = (
        frames == 1
        and 4 <= n <= MOST_DIRECT
        and n & (n - 1) == 0
        and HEADS % n == 0
        and positions % (8 * n) == 0
        and (rest == 0 or (LANES % rest == 0 and text * rest % (8 * LANES) == 0))
    )
    flat = [x.reshape(rows, width) for x in (tq, tk, tv, tc)]
    big = cost(40 * rows * text * width, 12 * rows * width)

    def swap(x, k):
        return lax.ppermute(x, AXIS, [(i, i ^ k) for i in range(n)])

    def cross(groups, *text_out):
        return pl.pallas_call(
            partial(cross_kernel, groups),
            out_shape=(bf16(rows, width),) + text_out,
            in_specs=[SMEM] + [VMEM] * 4,
            out_specs=(VMEM,) * (1 + len(text_out)),
            cost_estimate=big,
            compiler_params=PARAMS,
            name="cross",
        )(*cross_args)

    cross_args = (text_len, cq.reshape(rows, width), cc.reshape(rows, width), text_k, text_v)

    def temporal(messages, chunk, part, period, before, heights):
        count = len(messages)
        return pl.pallas_call(
            partial(temporal_kernel, count, chunk, part, period),
            out_shape=tuple(bf16(3, height, width) for height in heights),
            in_specs=[VMEM] * (count + len(before)),
            out_specs=(VMEM,) * count,
            cost_estimate=big,
            compiler_params=PARAMS,
        )(*messages, *before)

    if not direct:
        packed = jnp.stack(flat).reshape(4, frames, n, lanes, width).transpose(2, 0, 1, 3, 4)
        moved = lax.all_to_all(packed, AXIS, 0, 0, tiled=True)
        moved = moved.transpose(1, 0, 2, 3, 4).reshape(4, rows, width)
        tiles = 2 * width // LANES
        grad_cross, partials = cross(1, f32(1, tiles * text, LANES))
        partials = partials.reshape(tiles, text, LANES).transpose(1, 0, 2).reshape(text, -1)
        text_grad = lax.psum_scatter(partials, AXIS, scatter_dimension=1, tiled=True)
        (back,) = temporal([moved], 0, rows, lanes, [], [rows])
        back = back.reshape(3, n, frames, lanes, width).transpose(1, 0, 2, 3, 4)
        back = lax.all_to_all(back, AXIS, 0, 0, tiled=True)
        back = back.transpose(1, 2, 0, 3, 4).reshape(3, frames, positions, width)
        return back[0], back[1], back[2], grad_cross.reshape(cq.shape), text_grad

    each = positions // n
    chunks = CHUNKS if each % (8 * CHUNKS) == 0 else 1
    part = each // chunks
    near, far = range(n // 2), range(n // 2, n)
    plan = [(k, 0, each) for k in near] + [(k, c * part, part) for c in range(chunks) for k in far]
    messages = pl.pallas_call(
        partial(pack_kernel, each, plan),
        out_shape=tuple(bf16(4, height, width) for _, _, height in plan),
        in_specs=[HBM] * 4,
        out_specs=(VMEM,) * len(plan),
        scratch_shapes=[pltpu.SemaphoreType.DMA((len(plan), 4))],
        cost_estimate=cost(0, 16 * rows * width),
        compiler_params=PARAMS,
        name="pack",
    )(*[pltpu.with_memory_space_constraint(x, pltpu.HBM) for x in flat])
    messages, cross_args = lax.optimization_barrier((messages, cross_args))

    def exchange(plan, messages):
        moved = {}
        for (k, first, _), message in zip(plan, messages):
            moved[k, first // part] = swap(message, k) if k else message
        return moved

    came = exchange(plan, messages)

    high = text * columns // LANES
    grad_cross, stay, send = cross(n, f32(n // 2, high, LANES), bf16(n // 2, high, LANES))
    step = 1
    while True:
        got = swap(send, step)
        step *= 2
        if step == n:
            break
        both = stay + got.astype(jnp.float32)
        both = both.reshape(-1, 2, high, LANES)
        stay, send = both[:, 0], both[:, 1].astype(jnp.bfloat16)

    home, before = {}, []
    for c in range(chunks):
        last = c == chunks - 1
        got_now = [came[k, 0] for k in near] + [came[k, c] for k in far]
        heights = [each if last else part] * len(near) + [part] * len(far)
        back = temporal(got_now, c, part, part, before if last else [], heights)
        home |= exchange([(k, c * part, part) for k in far], back[len(near) :])
        if last:
            home |= exchange([(k, 0, each) for k in near], back[: len(near)])
        before += back[: len(near)]
    out = pl.pallas_call(
        partial(unpack_kernel, each, plan),
        out_shape=(bf16(rows, width),) * 3 + (f32(text, columns),),
        in_specs=[VMEM] * (len(plan) + 2),
        out_specs=(VMEM,) * 4,
        cost_estimate=cost(0, 12 * rows * width),
        compiler_params=PARAMS,
        name="unpack",
    )(*[home[k, first // part] for k, first, _ in plan], stay, got)
    return tuple(x.reshape(tq.shape) for x in out[:3]) + (grad_cross.reshape(cq.shape), out[3])


def solution(mesh):
    n = mesh.shape[AXIS]
    token = P(("clip", "seq"), None, None)

    def body(*args):
        return local(n, *args)

    step = jax.shard_map(
        body,
        mesh=mesh,
        in_specs=(token,) * 6 + (P("clip", None), P("clip", None), P("clip")),
        out_specs=(token,) * 4 + (P("clip", "seq"),),
        check_vma=False,
    )
    return step if 4 <= n <= MOST_DIRECT else step
```

```python
import math
from functools import partial

import jax
import jax.numpy as jnp
from jax import lax
from jax.experimental import pallas as pl
from jax.experimental.pallas import tpu as pltpu
from jax.sharding import PartitionSpec as P

HEADS = 16
LANES = 128
AXIS = "seq"
MOST_DIRECT = 8

CHUNKS = 2


VMEM = pl.BlockSpec(memory_space=pltpu.VMEM)
HBM = pl.BlockSpec(memory_space=pltpu.HBM)


def dot(a, b, along_a, along_b):
    dims = (((along_a,), (along_b,)), ((), ()))
    return lax.dot_general(a, b, dims, preferred_element_type=jnp.float32)


class Heads:
    def __init__(self, width):
        self.size = width // HEADS
        self.tiles = width // LANES
        self.masks = {}

    def mask(self, low, high):
        if (low, high) not in self.masks:
            lane = lax.broadcasted_iota(jnp.int32, (1, LANES), 1)
            inside = ((lane >= low) & (lane < high)).astype(jnp.float32)
            self.masks[low, high] = inside.astype(jnp.bfloat16)
        return self.masks[low, high]

    def touched(self, head):
        return range(head * self.size // LANES, -(-(head + 1) * self.size // LANES))

    def tile(self, x, t):
        return x[:, t * LANES : (t + 1) * LANES]

    def only(self, x, head, t):
        low = max(head * self.size - t * LANES, 0)
        high = min((head + 1) * self.size - t * LANES, LANES)
        return self.tile(x, t) * self.mask(low, high)

    def placed(self, x, head, to):
        start, out = head * self.size, {}
        for t in self.touched(head):
            turn = (to - start) % LANES
            turned = pltpu.roll(self.tile(x, t), turn, 1) if turn else self.tile(x, t)
            for u in range(to // LANES, -(-(to + self.size) // LANES)):
                low = max(0, LANES * t - start, LANES * u - to)
                high = min(self.size, LANES * (t + 1) - start, LANES * (u + 1) - to)
                if low < high:
                    part = turned * self.mask(to + low - LANES * u, to + high - LANES * u)
                    out[u] = out[u] + part if u in out else part
        return out

    def products(self, q, k, v, c, head):
        tiles = self.touched(head)
        ks = {t: self.only(k, head, t) for t in tiles}
        cs = {t: self.only(c, head, t) for t in tiles}
        scores = dot(beside(ks.values()), beside([self.tile(q, t) for t in tiles]), 1, 1)
        products = dot(beside([self.tile(v, t) for t in tiles]), beside(cs.values()), 1, 1)
        return scores, products, ks, cs


def beside(parts):
    parts = list(parts)
    return parts[0] if len(parts) == 1 else jnp.concatenate(parts, axis=1)


def below(parts):
    parts = list(parts)
    return parts[0] if len(parts) == 1 else jnp.concatenate(parts, axis=0)


def softmax_back(scores, products, keep, scale):
    scores = jnp.where(keep, scores, -1e30)
    expo = jnp.exp((scores - jnp.max(scores, axis=0, keepdims=True)) * scale)
    weights = expo * (1.0 / jnp.sum(expo, axis=0, keepdims=True))
    rounded = weights.astype(jnp.bfloat16)
    delta = jnp.sum(rounded.astype(jnp.float32) * products, axis=0, keepdims=True)
    return rounded, (weights * (products - delta) * scale).astype(jnp.bfloat16)


def attend_back(heads, q, k, v, c, keep, ahead, each_head, each_tile):
    scale = 1.0 / math.sqrt(heads.size)
    first, ready, tile = {}, {}, 0
    for step in range(HEADS + ahead):
        if step < HEADS:
            first[step] = heads.products(q, k, v, c, step)
        h = step - ahead
        if h < 0:
            continue
        scores, products, ks, cs = first.pop(h)
        rounded, sloped = softmax_back(scores, products, keep, scale)
        ready[h] = (rounded, sloped, ks, cs)
        each_head(h, rounded, sloped)
        while tile < heads.tiles and (tile + 1) * LANES <= (h + 1) * heads.size:
            parts = [
                (g, r, s, ks[tile], cs[tile])
                for g, (r, s, ks, cs) in sorted(ready.items())
                if tile in heads.touched(g)
            ]
            each_tile(tile, parts)
            ready = {g: x for g, x in ready.items() if heads.touched(g)[-1] > tile}
            tile += 1


def cross_kernel(groups, len_ref, q_ref, c_ref, k_ref, v_ref, grad_ref, *text_refs):
    rows, width = q_ref.shape
    text = k_ref.shape[0]
    heads = Heads(width)
    keep = lax.broadcasted_iota(jnp.int32, (text, rows), 0) < len_ref[...]
    q, c, k, v = q_ref[...], c_ref[...], k_ref[...], v_ref[...]
    per = HEADS // groups
    rest = 2 * per * heads.size % LANES
    terms, blocks = {}, []
    me = lax.axis_index(AXIS) if groups > 1 else 0

    def each_head(h, rounded, sloped):
        block, i = divmod(h, per)
        for left, x, to in ((sloped, q, 2 * i), (rounded, c, 2 * i + 1)):
            for t, value in heads.placed(x, h, to * heads.size).items():
                terms.setdefault(t, []).append((left, value))
        if i < per - 1:
            return
        tiles = [dot(beside(a for a, _ in x), below(b for _, b in x), 1, 0) for x in terms.values()]
        terms.clear()
        if rest:
            last, span = tiles.pop(), text * rest // LANES
            tiles.append(
                sum(
                    pltpu.roll(last[i * span : (i + 1) * span], i * rest, 1)
                    if i
                    else last[:span]
                    for i in range(LANES // rest)
                )
            )
        blocks.append(below(tiles))
        if groups == 1:
            text_refs[0][0] = blocks.pop()
        elif block % 2:
            odd, even = blocks.pop(), blocks.pop()
            place = (block // 2) ^ (me // 2)
            swapped = me % 2 == 1
            text_refs[0][place] = jnp.where(swapped, odd, even)
            text_refs[1][place] = jnp.where(swapped, even, odd).astype(jnp.bfloat16)

    def each_tile(t, parts):
        grad = dot(below(s for _, _, s, _, _ in parts), below(k for *_, k, _ in parts), 0, 0)
        grad_ref[:, t * LANES : (t + 1) * LANES] = grad.astype(jnp.bfloat16)

    attend_back(heads, q, k, v, c, keep, 6, each_head, each_tile)


def temporal_kernel(slots, chunk, part, period, *refs):
    ins, outs = refs[:slots], refs[-slots:]
    before = refs[slots:-slots]
    width = ins[0].shape[2]
    rows = part * slots
    heads = Heads(width)
    keep = (
        lax.broadcasted_iota(jnp.int32, (rows, rows), 0) % period
        == lax.broadcasted_iota(jnp.int32, (rows, rows), 1) % period
    )

    def mine(ref):
        return slice(None) if ref.shape[1] == part else slice(chunk * part, (chunk + 1) * part)

    q, k, v, c = (below(ref[t, mine(ref)] for ref in ins) for t in range(4))

    def product(left, right):
        if rows % LANES == 0:
            return dot(beside(left), below(right), 1, 0)
        return sum(dot(x, y, 1, 0) for x, y in zip(left, right))

    def each_tile(t, parts):
        slopes = [s for _, _, s, _, _ in parts]
        grads = (
            dot(below(slopes), below(k for *_, k, _ in parts), 0, 0),
            product(slopes, [heads.only(q, g, t) for g, *_ in parts]),
            product([r for _, r, *_ in parts], [c for *_, c in parts]),
        )
        for x, grad in enumerate(grads):
            grad = grad.astype(jnp.bfloat16)
            for i, ref in enumerate(outs):
                ref[x, mine(ref), t * LANES : (t + 1) * LANES] = grad[i * part : (i + 1) * part]

    whole = [ref for ref in outs if ref.shape[1] > part]
    for i, ref in enumerate(before):
        j, place = divmod(i, len(whole))
        whole[place][:, j * part : (j + 1) * part] = ref[...]
    attend_back(heads, q, k, v, c, keep, 8, lambda *_: None, each_tile)


def pack_kernel(each, plan, *refs):
    ins, outs, sems = refs[:4], refs[4:-1], refs[-1]
    me = lax.axis_index(AXIS)
    copies = []
    for i, ((k, first, rows), out) in enumerate(zip(plan, outs)):
        start = pl.multiple_of((me ^ k) * each + first, 8)
        for t, ref in enumerate(ins):
            copies.append(
                pltpu.make_async_copy(ref.at[pl.ds(start, rows)], out.at[t], sems.at[i, t])
            )
    for copy in copies:
        copy.start()
    for copy in copies:
        copy.wait()


def unpack_kernel(each, plan, *refs):
    count = len(plan)
    ins, (kept, got), outs = refs[:count], refs[count : count + 2], refs[count + 2 :]
    me = lax.axis_index(AXIS)
    for (k, first, rows), ref in zip(plan, ins):
        start = pl.multiple_of((me ^ k) * each + first, 8)
        for t in range(3):
            outs[t][pl.ds(start, rows), :] = ref[t]
    total = kept[0] + got[0].astype(jnp.float32)
    text, columns = outs[3].shape
    whole, rest = divmod(columns, LANES)
    for t in range(whole):
        outs[3][:, t * LANES : (t + 1) * LANES] = total[t * text : (t + 1) * text]
    span = text * rest // LANES
    for i in range(LANES // rest if rest else 0):
        last = total[whole * text : whole * text + span, i * rest : (i + 1) * rest]
        outs[3][i * span : (i + 1) * span, whole * LANES :] = last


PARAMS = pltpu.CompilerParams(vmem_limit_bytes=8 << 20)


def cost(flops, moved):
    return pl.CostEstimate(flops=int(flops), bytes_accessed=int(moved), transcendentals=0)


def bf16(*shape):
    return jax.ShapeDtypeStruct(shape, jnp.bfloat16)


def f32(*shape):
    return jax.ShapeDtypeStruct(shape, jnp.float32)


def halved(n):
    return range(n // 2, n)


def local(n, tq, tk, tv, tc, cq, cc, text_k, text_v, text_len):
    frames, positions, width = tq.shape
    rows = frames * positions
    text = text_k.shape[0]
    lanes = positions // n
    columns = 2 * width // n
    rest = columns % LANES
    direct = (
        frames == 1
        and 4 <= n <= MOST_DIRECT
        and n & (n - 1) == 0
        and HEADS % n == 0
        and positions % (8 * n) == 0
        and (rest == 0 or (LANES % rest == 0 and text * rest % (8 * LANES) == 0))
    )
    flat = [x.reshape(rows, width) for x in (tq, tk, tv, tc)]
    big = cost(40 * rows * text * width, 12 * rows * width)

    def swap(x, k):
        return lax.ppermute(x, AXIS, [(i, i ^ k) for i in range(n)])

    def cross(groups, *text_out):
        return pl.pallas_call(
            partial(cross_kernel, groups),
            out_shape=(bf16(rows, width),) + text_out,
            in_specs=[VMEM] * 5,
            out_specs=(VMEM,) * (1 + len(text_out)),
            cost_estimate=big,
            compiler_params=PARAMS,
            name="cross",
        )(*cross_args)

    cross_args = (text_len.reshape(1, 1), cq.reshape(rows, width), cc.reshape(rows, width), text_k, text_v)

    def temporal(messages, chunk, part, period, before, heights):
        count = len(messages)
        return pl.pallas_call(
            partial(temporal_kernel, count, chunk, part, period),
            out_shape=tuple(bf16(3, height, width) for height in heights),
            in_specs=[VMEM] * (count + len(before)),
            out_specs=(VMEM,) * count,
            cost_estimate=big,
            compiler_params=PARAMS,
        )(*messages, *before)

    if not direct:
        packed = jnp.stack(flat).reshape(4, frames, n, lanes, width).transpose(2, 0, 1, 3, 4)
        moved = lax.all_to_all(packed, AXIS, 0, 0, tiled=True)
        moved = moved.transpose(1, 0, 2, 3, 4).reshape(4, rows, width)
        tiles = 2 * width // LANES
        grad_cross, partials = cross(1, f32(1, tiles * text, LANES))
        partials = partials.reshape(tiles, text, LANES).transpose(1, 0, 2).reshape(text, -1)
        text_grad = lax.psum_scatter(partials, AXIS, scatter_dimension=1, tiled=True)
        (back,) = temporal([moved], 0, rows, lanes, [], [rows])
        back = back.reshape(3, n, frames, lanes, width).transpose(1, 0, 2, 3, 4)
        back = lax.all_to_all(back, AXIS, 0, 0, tiled=True)
        back = back.transpose(1, 2, 0, 3, 4).reshape(3, frames, positions, width)
        return back[0], back[1], back[2], grad_cross.reshape(cq.shape), text_grad

    each = positions // n
    chunks = CHUNKS if each % (8 * CHUNKS) == 0 else 1
    part = each // chunks
    near = [k for k in range(n) if k not in halved(n)]
    far = list(halved(n))
    plan = [(k, 0, each) for k in near] + [(k, c * part, part) for c in range(chunks) for k in far]
    messages = pl.pallas_call(
        partial(pack_kernel, each, plan),
        out_shape=tuple(bf16(4, height, width) for _, _, height in plan),
        in_specs=[HBM] * 4,
        out_specs=(VMEM,) * len(plan),
        scratch_shapes=[pltpu.SemaphoreType.DMA((len(plan), 4))],
        cost_estimate=cost(0, 16 * rows * width),
        compiler_params=PARAMS,
        name="pack",
    )(*[pltpu.with_memory_space_constraint(x, pltpu.HBM) for x in flat])
    messages, cross_args = lax.optimization_barrier((messages, cross_args))

    def exchange(plan, messages):
        moved = {}
        for (k, first, _), message in zip(plan, messages):
            moved[k, first // part] = swap(message, k) if k else message
        return moved

    came = exchange(plan, messages)

    high = text * columns // LANES
    grad_cross, stay, send = cross(n, f32(n // 2, high, LANES), bf16(n // 2, high, LANES))
    step = 1
    while True:
        got = swap(send, step)
        step *= 2
        if step == n:
            break
        both = stay + got.astype(jnp.float32)
        both = both.reshape(-1, 2, high, LANES)
        stay, send = both[:, 0], both[:, 1].astype(jnp.bfloat16)

    home, before = {}, []
    for c in range(chunks):
        last = c == chunks - 1
        got_now = [came[k, 0] for k in near] + [came[k, c] for k in far]
        heights = [each if last else part] * len(near) + [part] * len(far)
        back = temporal(got_now, c, part, part, before if last else [], heights)
        home |= exchange([(k, c * part, part) for k in far], back[len(near) :])
        if last:
            home |= exchange([(k, 0, each) for k in near], back[: len(near)])
        before += back[: len(near)]
    out = pl.pallas_call(
        partial(unpack_kernel, each, plan),
        out_shape=(bf16(rows, width),) * 3 + (f32(text, columns),),
        in_specs=[VMEM] * (len(plan) + 2),
        out_specs=(VMEM,) * 4,
        cost_estimate=cost(0, 12 * rows * width),
        compiler_params=PARAMS,
        name="unpack",
    )(*[home[k, first // part] for k, first, _ in plan], stay, got)
    return tuple(x.reshape(tq.shape) for x in out[:3]) + (grad_cross.reshape(cq.shape), out[3])


def solution(mesh):
    n = mesh.shape[AXIS]
    token = P(("clip", "seq"), None, None)

    def body(*args):
        return local(n, *args)

    step = jax.shard_map(
        body,
        mesh=mesh,
        in_specs=(token,) * 6 + (P("clip", None), P("clip", None), P("clip")),
        out_specs=(token,) * 4 + (P("clip", "seq"),),
        check_vma=False,
    )
    return step if 4 <= n <= MOST_DIRECT else step
```
